32 devices in a mesh: dp: 8 (over y, x, core), tensor: 4 (over z).
Axes of the slice: x: 2, y: 2, z: 4, core: 2. Of those that a mesh axis runs over, the one named last changes fastest.
Arguments:
- block_input: bfloat16 [4096, 1024], P(('dp', 'tensor')), may hold values from -6 to 6
- norm1_gain: float32 [1024], replicated, may hold values from 0.25 to 1.75
- norm1_bias: float32 [1024], replicated, may hold values from -3 to 3
- qkv_weight: bfloat16 [1024, 3, 512], P(None, None, 'tensor')
- qkv_bias: float32 [2, 512], P(None, 'tensor'), may hold values from -3 to 3
- out_weight: bfloat16 [512, 1024], P('tensor'), may hold values from -0.75 to 0.75
- out_bias: float32 [1024], replicated, may hold values from -3 to 3
- norm2_gain: float32 [1024], replicated, may hold values from 0.25 to 1.75
- norm2_bias: float32 [1024], replicated, may hold values from -3 to 3
- up_weight: bfloat16 [1024, 2048], P(None, 'tensor'), may hold values from -0.1875 to 0.1875
- up_bias: float32 [2048], P('tensor'), may hold values from -3 to 3
- down_weight: bfloat16 [2048, 1024], P('tensor'), may hold values from -0.125 to 0.125
- down_bias: float32 [1024], replicated, may hold values from -3 to 3
- lengths: int32 [32], replicated, may hold values from 1 to 509, as said below
- seq_owner: int32 [32], replicated, may hold values from 0 to 7, as said below
- cotangent: bfloat16 [4096, 1024], P(('dp', 'tensor')), may hold values from -6 to 6
Outputs:
- block_output: bfloat16 [4096, 1024], P(('dp', 'tensor'))
- input_grad: bfloat16 [4096, 1024], P(('dp', 'tensor'))
- grad_norm1_gain: float32 [1024], replicated
- grad_norm1_bias: float32 [1024], replicated
- grad_qkv_weight: float32 [1024, 3, 512], P(None, None, 'tensor')
- grad_qkv_bias: float32 [2, 512], P(None, 'tensor')
- grad_out_weight: float32 [512, 1024], P('tensor')
- grad_out_bias: float32 [1024], replicated
- grad_norm2_gain: float32 [1024], replicated
- grad_norm2_bias: float32 [1024], replicated
- grad_up_weight: float32 [1024, 2048], P(None, 'tensor')
- grad_up_bias: float32 [2048], P('tensor')
- grad_down_weight: float32 [2048, 1024], P('tensor')
- grad_down_bias: float32 [1024], replicated
The draws below stay inside these ranges and needn't reach their ends.
Inputs may be any that keep to these rules, and one draw needn't show every extreme that they name: `seq_owner`: each index of dp owns exactly 4 sequences. The lengths of the sequences owned by one index of dp sum to at most 512, and to exactly 512 for some index of dp in every draw.
All inputs are finite; a program needn't handle non-finite values.
Results may differ from the reference program's by a relative error of at most 0.011.
Values may be sent and summed in bfloat16 or wider, within the bound.
No kernel may reach another device: no remote copies, remote signals or barrier semaphores. Data moves between devices by JAX's collectives and lax.ppermute only.
A program may use at most 64 MiB of HBM per device.

```python
import math
import jax
import jax.numpy as jnp
from jax import lax

D = 1024
HEADS = 8
HD = 64
FF = 2048
TOK_DEV = 512
SEQ_DEV = 4
TOKENS = 4096
SEQS = 32
N_DP = 8


def deal_sequences(key):
    base_key = jax.random.fold_in(key, 7)
    key_totals, key_full, key_cuts, key_order = jax.random.split(base_key, 4)
    device_count = SEQS // SEQ_DEV
    totals = jax.random.randint(key_totals, (device_count,), TOK_DEV // 4, TOK_DEV + 1)
    full_device = jax.random.randint(key_full, (), 0, device_count)
    is_full = jnp.arange(device_count) == full_device
    totals = jnp.where(is_full, TOK_DEV, totals).astype(jnp.int32)
    spare = totals - SEQ_DEV
    cut_draw = jax.random.randint(key_cuts, (device_count, SEQ_DEV - 1), 0, TOK_DEV)
    cut_points = jnp.sort(cut_draw % (spare + 1)[:, None], axis=1)
    cut_points = jnp.where(is_full[:, None], spare[:, None], cut_points)
    edges = jnp.concatenate([jnp.zeros((device_count, 1), jnp.int32), cut_points.astype(jnp.int32), spare[:, None]], axis=1)
    pieces = edges[:, 1:] - edges[:, :-1] + 1
    order = jax.random.permutation(key_order, SEQS)
    owner_of = jnp.zeros((SEQS,), jnp.int32).at[order].set((jnp.arange(SEQS) // SEQ_DEV).astype(jnp.int32))
    length_of = jnp.zeros((SEQS,), jnp.int32).at[order].set(pieces.reshape(-1).astype(jnp.int32))
    return (length_of, owner_of)


def draw_lengths(key, part):
    return deal_sequences(key)[0]


def draw_seq_owner(key, part):
    return deal_sequences(key)[1]


def draw_qkv_weight(key, part):
    key_base = jax.random.fold_in(jax.random.fold_in(key, 11), 0)
    weights = jnp.clip(jax.random.normal(key_base, (D, 3, HEADS * HD), jnp.float32), -6.0, 6.0) / math.sqrt(D)
    return weights.astype(jnp.bfloat16)


def levels(rng, extent, cuts, least, high):
    level, own = 1.0, jax.random.fold_in(rng, 6)
    for axis_at, parts in cuts:
        draws = jnp.exp(jax.random.uniform(jax.random.fold_in(own, axis_at), (parts,), jnp.float32, least / len(cuts), high / len(cuts)))
        level = level * jnp.repeat(draws, extent[axis_at] // parts).reshape([-1 if axis == axis_at else 1 for axis in range(len(extent))])
    return level


def scatter_about(own_key, extent, spread, reach, shards=(), held_as=jnp.bfloat16):
    level = levels(own_key, extent, shards, -0.22, 0.18) if shards else 1.0
    drawn = jax.random.normal(own_key, extent, jnp.float32) * spread * level
    return jnp.minimum(jnp.maximum(drawn, -reach), reach).astype(held_as)


def setup_inputs(seed: int = 0) -> dict:
    streams_of = jax.random.split(jax.random.key(seed), 17)
    block_input = scatter_about(streams_of[0], (TOKENS, D), 1.0, 6.0, ((0, 32),))
    norm1_gain = jnp.clip(1.0 + 0.15 * jax.random.normal(streams_of[1], (D,), jnp.float32), 0.25, 1.75)
    norm1_bias = scatter_about(streams_of[2], (D,), 0.5, 3.0, (), jnp.float32)
    qkv_weight = draw_qkv_weight(jax.random.fold_in(streams_of[16], 71), 0)
    qkv_bias = scatter_about(streams_of[4], (2, HEADS * HD), 0.5, 3.0, ((1, 4),), jnp.float32)
    out_weight = scatter_about(streams_of[5], (HEADS * HD, D), HD ** -0.5, 0.75, ((0, 4),))
    out_bias = scatter_about(streams_of[6], (D,), 0.5, 3.0, (), jnp.float32)
    norm2_gain = jnp.clip(1.0 + 0.15 * jax.random.normal(streams_of[7], (D,), jnp.float32), 0.25, 1.75)
    norm2_bias = scatter_about(streams_of[8], (D,), 0.5, 3.0, (), jnp.float32)
    up_weight = scatter_about(streams_of[9], (D, FF), D ** -0.5, 0.1875, ((1, 4),))
    up_bias = scatter_about(streams_of[10], (FF,), 0.5, 3.0, ((0, 4),), jnp.float32)
    down_weight = scatter_about(streams_of[11], (FF, D), FF ** -0.5, 0.125, ((0, 4),))
    down_bias = scatter_about(streams_of[12], (D,), 0.5, 3.0, (), jnp.float32)
    lengths = draw_lengths(jax.random.fold_in(streams_of[16], 71), 0)
    seq_owner = draw_seq_owner(jax.random.fold_in(streams_of[16], 71), 0)
    cotangent = scatter_about(streams_of[15], (TOKENS, D), 1.0, 6.0, ((0, 32),))
    return {"block_input": block_input, "norm1_gain": norm1_gain, "norm1_bias": norm1_bias, "qkv_weight": qkv_weight, "qkv_bias": qkv_bias, "out_weight": out_weight, "out_bias": out_bias, "norm2_gain": norm2_gain, "norm2_bias": norm2_bias, "up_weight": up_weight, "up_bias": up_bias, "down_weight": down_weight, "down_bias": down_bias, "lengths": lengths, "seq_owner": seq_owner, "cotangent": cotangent}


gelu_scale = 0.7978845608028654
gelu_cubic = 0.044715

def gelu_value(pre_act):
    inner = jnp.tanh(gelu_scale * (pre_act + gelu_cubic * pre_act * pre_act * pre_act))
    return 0.5 * pre_act * (1.0 + inner)

def gelu_slope(pre_act):
    inner = jnp.tanh(gelu_scale * (pre_act + gelu_cubic * pre_act * pre_act * pre_act))
    return 0.5 * (1.0 + inner) + 0.5 * pre_act * (1.0 - inner * inner) * gelu_scale * (1.0 + 3.0 * gelu_cubic * pre_act * pre_act)

def normalize(values):
    center = lax.optimization_barrier(jnp.mean(values, axis=-1, keepdims=True))
    shifted = values - center
    variance = lax.optimization_barrier(jnp.mean(shifted * shifted, axis=-1, keepdims=True))
    inv_std = lax.rsqrt(variance + 1e-05)
    return (shifted * inv_std, inv_std)

def norm_back(grad_in, normed, inv_std, gain):
    scaled = grad_in * gain
    return inv_std * (scaled - lax.optimization_barrier(jnp.mean(scaled, axis=-1, keepdims=True)) - normed * lax.optimization_barrier(jnp.mean(scaled * normed, axis=-1, keepdims=True)))

def layout_ids(lengths, seq_owner, device, slot_count):
    owned = seq_owner == device
    owned_lengths = jnp.where(owned, lengths, 0).astype(jnp.int32)
    seq_starts = (jnp.cumsum(owned_lengths) - owned_lengths).astype(jnp.int32)
    slot_index = jnp.arange(slot_count, dtype=jnp.int32)
    members = owned[:, None] & (slot_index[None, :] >= seq_starts[:, None]) & (slot_index[None, :] < (seq_starts + owned_lengths)[:, None])
    labels = jnp.arange(1, lengths.shape[0] + 1, dtype=jnp.int32)
    return lax.optimization_barrier(jnp.sum(jnp.where(members, labels[:, None], 0), axis=0)).astype(jnp.int32)

def score_table(raw_scores, slopes, sequence_ids):
    slot_count = raw_scores.shape[-1]
    positions = jnp.arange(slot_count).astype(jnp.float32)
    distance = positions[:, None] - positions[None, :]
    allowed = (sequence_ids[:, None] == sequence_ids[None, :]) & (distance >= 0.0)
    scores = raw_scores * 0.125 - slopes[:, None, None] * distance[None, :, :]
    return (jnp.where(allowed[None], scores, -1e+30), allowed)

def attend(query, keys, values, slopes, sequence_ids):
    raw_scores = jnp.einsum('ihd,jhd->hij', query.astype(jnp.float32), keys.astype(jnp.float32))
    scores, allowed = score_table(raw_scores, slopes, sequence_ids)
    maximum = lax.optimization_barrier(jnp.max(scores, axis=-1, keepdims=True))
    log_total = maximum + jnp.log(lax.optimization_barrier(jnp.sum(jnp.exp(scores - maximum), axis=-1, keepdims=True)))
    prob_bf = jnp.where(allowed[None], jnp.exp(scores - log_total), 0.0).astype(jnp.bfloat16)
    context = jnp.einsum('hij,jhd->ihd', prob_bf.astype(jnp.float32), values.astype(jnp.float32)).astype(jnp.bfloat16)
    return (context, log_total)

def attend_back(query, keys, values, slopes, sequence_ids, log_total, context_grad):
    raw_scores = jnp.einsum('ihd,jhd->hij', query.astype(jnp.float32), keys.astype(jnp.float32))
    scores, allowed = score_table(raw_scores, slopes, sequence_ids)
    probs = jnp.where(allowed[None], jnp.exp(scores - log_total), 0.0)
    prob_bf = probs.astype(jnp.bfloat16)
    prob_grad = jnp.einsum('ihd,jhd->hij', context_grad.astype(jnp.float32), values.astype(jnp.float32))
    row_delta = lax.optimization_barrier(jnp.sum(probs * prob_grad, axis=-1, keepdims=True))
    score_grad = (probs * (prob_grad - row_delta)).astype(jnp.bfloat16)
    query_grad = (jnp.einsum('hij,jhd->ihd', score_grad.astype(jnp.float32), keys.astype(jnp.float32)) * 0.125).astype(jnp.bfloat16)
    key_grad = (jnp.einsum('hij,ihd->jhd', score_grad.astype(jnp.float32), query.astype(jnp.float32)) * 0.125).astype(jnp.bfloat16)
    value_grad = jnp.einsum('hij,ihd->jhd', prob_bf.astype(jnp.float32), context_grad.astype(jnp.float32)).astype(jnp.bfloat16)
    return (query_grad, key_grad, value_grad)

def reference(block_input, norm1_gain, norm1_bias, qkv_weight, qkv_bias, out_weight, out_bias, norm2_gain, norm2_bias, up_weight, up_bias, down_weight, down_bias, lengths, seq_owner, cotangent):
    head_width = HEADS * HD
    qkv_flat = qkv_weight.reshape(D, 3 * head_width)
    qkv_shift = jnp.concatenate([qkv_bias[0], jnp.zeros((head_width,), jnp.float32), qkv_bias[1]])
    slopes = jnp.exp2(-8.0 * (jnp.arange(HEADS) + 1).astype(jnp.float32) / HEADS)
    inputs_all = block_input.reshape(N_DP, TOK_DEV, D)
    cot_all = cotangent.reshape(N_DP, TOK_DEV, D)
    devices = jnp.arange(N_DP, dtype=jnp.int32)

    def one_block(totals, item):
        input_rows, cot_rows, device = item
        sequence_ids = layout_ids(lengths, seq_owner, device, TOK_DEV)
        live_rows = (sequence_ids > 0).astype(jnp.float32)[:, None]
        input_float = input_rows.astype(jnp.float32)
        normed1, inv_std1 = normalize(input_float)
        norm1_out = (normed1 * norm1_gain + norm1_bias).astype(jnp.bfloat16)
        projected = (jnp.dot(norm1_out, qkv_flat, preferred_element_type=jnp.float32) + qkv_shift).astype(jnp.bfloat16)
        split_qkv = projected.reshape(TOK_DEV, 3, HEADS, HD)
        query, keys, values = (split_qkv[:, 0], split_qkv[:, 1], split_qkv[:, 2])
        context, log_total = attend(query, keys, values, slopes, sequence_ids)
        context_flat = context.reshape(TOK_DEV, head_width)
        residual = input_float + (jnp.dot(context_flat, out_weight, preferred_element_type=jnp.float32) + out_bias)
        normed2, inv_std2 = normalize(residual)
        norm2_out = (normed2 * norm2_gain + norm2_bias).astype(jnp.bfloat16)
        pre_act = jnp.dot(norm2_out, up_weight, preferred_element_type=jnp.float32) + up_bias
        activated = gelu_value(pre_act).astype(jnp.bfloat16)
        ffn_out = jnp.dot(activated, down_weight, preferred_element_type=jnp.float32) + down_bias
        block_output = (live_rows * (residual + ffn_out)).astype(jnp.bfloat16)
        grad_out = live_rows * cot_rows.astype(jnp.float32)
        grad_out_bf = grad_out.astype(jnp.bfloat16)
        act_grad = jnp.dot(grad_out_bf, down_weight.T, preferred_element_type=jnp.float32)
        pre_grad = (act_grad * gelu_slope(pre_act)).astype(jnp.bfloat16)
        grad_down_weight = jnp.dot(activated.T, grad_out_bf, preferred_element_type=jnp.float32)
        grad_down_bias = lax.optimization_barrier(jnp.sum(grad_out, axis=0))
        grad_up_weight = jnp.dot(norm2_out.T, pre_grad, preferred_element_type=jnp.float32)
        grad_up_bias = lax.optimization_barrier(jnp.sum(pre_grad.astype(jnp.float32), axis=0))
        norm2_grad = jnp.dot(pre_grad, up_weight.T, preferred_element_type=jnp.float32)
        grad_norm2_gain = lax.optimization_barrier(jnp.sum(norm2_grad * normed2, axis=0))
        grad_norm2_bias = lax.optimization_barrier(jnp.sum(norm2_grad, axis=0))
        resid_grad = grad_out + norm_back(norm2_grad, normed2, inv_std2, norm2_gain)
        grad_out_bias = lax.optimization_barrier(jnp.sum(resid_grad, axis=0))
        resid_grad_bf = resid_grad.astype(jnp.bfloat16)
        grad_out_weight = jnp.dot(context_flat.T, resid_grad_bf, preferred_element_type=jnp.float32)
        context_grad = jnp.dot(resid_grad_bf, out_weight.T, preferred_element_type=jnp.float32).astype(jnp.bfloat16).reshape(TOK_DEV, HEADS, HD)
        query_grad, key_grad, value_grad = attend_back(query, keys, values, slopes, sequence_ids, log_total, context_grad)
        query_flat = query_grad.reshape(TOK_DEV, head_width)
        value_flat = value_grad.reshape(TOK_DEV, head_width)
        qkv_grad = jnp.stack([query_flat, key_grad.reshape(TOK_DEV, head_width), value_flat], axis=1).reshape(TOK_DEV, 3 * head_width)
        grad_qkv_weight = jnp.dot(norm1_out.T, qkv_grad, preferred_element_type=jnp.float32).reshape(D, 3, head_width)
        grad_qkv_bias = jnp.stack([lax.optimization_barrier(jnp.sum(query_flat.astype(jnp.float32), axis=0)), lax.optimization_barrier(jnp.sum(value_flat.astype(jnp.float32), axis=0))])
        norm1_grad = jnp.dot(qkv_grad, qkv_flat.T, preferred_element_type=jnp.float32)
        grad_norm1_gain = lax.optimization_barrier(jnp.sum(norm1_grad * normed1, axis=0))
        grad_norm1_bias = lax.optimization_barrier(jnp.sum(norm1_grad, axis=0))
        input_grad = (resid_grad + norm_back(norm1_grad, normed1, inv_std1, norm1_gain)).astype(jnp.bfloat16)
        grads = (grad_norm1_gain, grad_norm1_bias, grad_qkv_weight, grad_qkv_bias, grad_out_weight, grad_out_bias, grad_norm2_gain, grad_norm2_bias, grad_up_weight, grad_up_bias, grad_down_weight, grad_down_bias)
        return (jax.tree.map(jnp.add, totals, grads), (block_output, input_grad))
    zero_grads = (jnp.zeros((D,), jnp.float32), jnp.zeros((D,), jnp.float32), jnp.zeros((D, 3, head_width), jnp.float32), jnp.zeros((2, head_width), jnp.float32), jnp.zeros((head_width, D), jnp.float32), jnp.zeros((D,), jnp.float32), jnp.zeros((D,), jnp.float32), jnp.zeros((D,), jnp.float32), jnp.zeros((D, FF), jnp.float32), jnp.zeros((FF,), jnp.float32), jnp.zeros((FF, D), jnp.float32), jnp.zeros((D,), jnp.float32))
    totals, outputs = lax.scan(one_block, zero_grads, (inputs_all, cot_all, devices))
    block_output = outputs[0].reshape(TOKENS, D)
    input_grad = outputs[1].reshape(TOKENS, D)
    return (block_output, input_grad, totals[0], totals[1], totals[2], totals[3], totals[4], totals[5], totals[6], totals[7], totals[8], totals[9], totals[10], totals[11])
```

```python
import jax
import jax.numpy as jnp
from jax import lax
from jax.sharding import PartitionSpec as P

HEADS = 8
HD = 64


bf16 = jnp.bfloat16
f32 = jnp.float32

gelu_scale = 0.7978845608028654
gelu_cubic = 0.044715


def gelu_both(pre_act):
    square = pre_act * pre_act
    inner = jnp.tanh(gelu_scale * (pre_act + gelu_cubic * pre_act * square))
    value = 0.5 * pre_act * (1.0 + inner)
    slope = 0.5 * (1.0 + inner) + 0.5 * pre_act * (1.0 - inner * inner) * gelu_scale * (
        1.0 + 3.0 * gelu_cubic * square
    )
    return value, slope


def normalize(values):
    center = jnp.mean(values, axis=-1, keepdims=True)
    shifted = values - center
    variance = jnp.mean(shifted * shifted, axis=-1, keepdims=True)
    inv_std = lax.rsqrt(variance + 1e-05)
    return (shifted * inv_std, inv_std)


def norm_back(grad_in, normed, inv_std, gain):
    scaled = grad_in * gain
    return inv_std * (
        scaled
        - jnp.mean(scaled, axis=-1, keepdims=True)
        - normed * jnp.mean(scaled * normed, axis=-1, keepdims=True)
    )


def ids_at(lengths, seq_owner, device, slots):
    owned = seq_owner == device
    owned_lengths = jnp.where(owned, lengths, 0)
    seq_starts = jnp.cumsum(owned_lengths) - owned_lengths
    members = (
        owned[:, None]
        & (slots[None, :] >= seq_starts[:, None])
        & (slots[None, :] < (seq_starts + owned_lengths)[:, None])
    )
    labels = jnp.arange(1, lengths.shape[0] + 1, dtype=jnp.int32)
    return jnp.sum(jnp.where(members, labels[:, None], 0), axis=0)


def score_table(raw_scores, slopes, positions, sequence_ids):
    distance = positions[:, None] - positions[None, :]
    allowed = (sequence_ids[:, None] == sequence_ids[None, :]) & (distance >= 0.0)
    scores = raw_scores * 0.125 - slopes[:, None, None] * distance[None, :, :]
    return (jnp.where(allowed[None], scores, -1e30), allowed)


def attend(query, keys, values, slopes, positions, sequence_ids):
    raw_scores = jnp.einsum("ihd,jhd->hij", query, keys, preferred_element_type=f32)
    scores, allowed = score_table(raw_scores, slopes, positions, sequence_ids)
    maximum = jnp.max(scores, axis=-1, keepdims=True)
    log_total = maximum + jnp.log(jnp.sum(jnp.exp(scores - maximum), axis=-1, keepdims=True))
    prob_bf = jnp.where(allowed[None], jnp.exp(scores - log_total), 0.0).astype(bf16)
    context = jnp.einsum("hij,jhd->ihd", prob_bf, values, preferred_element_type=f32).astype(bf16)
    return (context, log_total)


def attend_back(query, keys, values, slopes, positions, sequence_ids, log_total, context_grad):
    raw_scores = jnp.einsum("ihd,jhd->hij", query, keys, preferred_element_type=f32)
    scores, allowed = score_table(raw_scores, slopes, positions, sequence_ids)
    probs = jnp.where(allowed[None], jnp.exp(scores - log_total), 0.0)
    prob_bf = probs.astype(bf16)
    prob_grad = jnp.einsum("ihd,jhd->hij", context_grad, values, preferred_element_type=f32)
    row_delta = jnp.sum(probs * prob_grad, axis=-1, keepdims=True)
    score_grad = (probs * (prob_grad - row_delta)).astype(bf16)
    query_grad = (
        jnp.einsum("hij,jhd->ihd", score_grad, keys, preferred_element_type=f32) * 0.125
    ).astype(bf16)
    key_grad = (
        jnp.einsum("hij,ihd->jhd", score_grad, query, preferred_element_type=f32) * 0.125
    ).astype(bf16)
    value_grad = jnp.einsum(
        "hij,ihd->jhd", prob_bf, context_grad, preferred_element_type=f32
    ).astype(bf16)
    return (query_grad, key_grad, value_grad)


def dot_first(left, right):
    return lax.dot_general(left, right, (((0,), (0,)), ((), ())), preferred_element_type=f32)


def dot_last(left, right):
    return lax.dot_general(left, right, (((1,), (1,)), ((), ())), preferred_element_type=f32)


def dot_plain(left, right):
    return lax.dot_general(left, right, (((1,), (0,)), ((), ())), preferred_element_type=f32)


def after(value, *events):
    return lax.optimization_barrier((value,) + events)[0]


class Ring:
    def __init__(self):
        self.size = lax.axis_size("tensor")
        self.own = lax.axis_index("tensor")
        half = self.size // 2
        self.order = sorted(range(1, self.size), key=lambda k: abs(k - half))

    def _move(self, value, shift):
        pairs = [(i, (i + shift) % self.size) for i in range(self.size)]
        return lax.ppermute(value, "tensor", pairs)

    def gather(self, value):
        got = {k: self._move(value, k) for k in self.order}
        return [value] + [got[k] for k in range(1, self.size)]

    def scatter(self, blocks):
        got = {k: self._move(blocks[k], -k) for k in self.order}
        back = [blocks[0]] + [got[k] for k in range(1, self.size)]
        return [back[-k % self.size] for k in range(self.size)]


class Plane:
    def __init__(self):
        self.count = lax.axis_size("dp")
        self.cores = 2 if self.count % 2 == 0 else 1
        rest = self.count // self.cores
        self.units = 4 if rest % 4 == 0 else 2 if rest % 2 == 0 else 1
        self.group = self.cores * self.units
        self.outer = self.count // self.group
        index = lax.axis_index("dp")
        self.core = index % self.cores
        self.unit = (index // self.cores) % self.units
        self.member = index % self.group
        self.order = sorted(range(1, self.units), reverse=True)

    def _move(self, value, flip):
        return lax.ppermute(value, "dp", [(i, i ^ flip) for i in range(self.count)])

    def swap(self, value):
        return self._move(value, 1)

    def gather(self, value):
        got = {k: self._move(value, k * self.cores) for k in self.order}
        return [value] + [got[k] for k in range(1, self.units)]

    def scatter(self, blocks):
        got = {k: self._move(blocks[k], k * self.cores) for k in self.order}
        return [blocks[0]] + [got[k] for k in range(1, self.units)]

    def outer_sum(self, value):
        if self.outer & (self.outer - 1):
            spans = [
                [o * self.group + m for o in range(self.outer)] for m in range(self.group)
            ]
            return lax.psum(value, "dp", axis_index_groups=spans)
        step = self.group
        while step < self.count:
            value = value + self._move(value, step)
            step *= 2
        return value

    def core_parts(self, pair):
        if self.cores == 1:
            return pair[0], pair[1]
        first = self.core == 0
        return jnp.where(first, pair[0], pair[1]), jnp.where(first, pair[1], pair[0])

    def reduce_pieces(self, pieces):
        split = pieces.reshape((self.units, self.cores) + pieces.shape[1:])
        if self.cores == 2:
            keep, give = self.core_parts((split[:, 0], split[:, 1]))
            keep = keep + self.swap(give.astype(bf16)).astype(f32)
        else:
            keep = split[:, 0]
        blocks = [
            lax.dynamic_index_in_dim(keep, self.unit ^ k, 0, keepdims=False)
            for k in range(self.units)
        ]
        return self.sum_blocks(blocks)

    def sum_blocks(self, blocks):
        got = self.scatter([blocks[0]] + [b.astype(bf16) for b in blocks[1:]])
        return sum((g.astype(f32) for g in got[1:]), got[0])

    def gather_pieces(self, piece):
        near = self.gather(piece)
        if self.cores == 1:
            return near
        far = [self.swap(value) for value in near]
        return [value for pair in zip(near, far) for value in pair]

    def in_order(self, pieces, own, convert):
        rows = pieces[0].shape[0]
        first = convert(pieces[0])
        total = jnp.zeros((rows * len(pieces),) + first.shape[1:], first.dtype)
        for k, piece in enumerate(pieces):
            total = lax.dynamic_update_slice_in_dim(total, convert(piece), (own ^ k) * rows, 0)
        return total


def sum_ring(ring, blocks):
    got = ring.scatter([blocks[0]] + [b.astype(bf16) for b in blocks[1:]])
    return sum((g.astype(f32) for g in got[1:]), got[0])


def shards(
    block_input,
    norm1_gain,
    norm1_bias,
    qkv_weight,
    qkv_bias,
    out_weight,
    out_bias,
    norm2_gain,
    norm2_bias,
    up_weight,
    up_bias,
    down_weight,
    down_bias,
    lengths,
    seq_owner,
    cotangent,
):
    ring, plane = Ring(), Plane()
    rows, width = block_input.shape
    parts, units, group = ring.size, plane.units, plane.group
    head_width = qkv_weight.shape[2]
    heads_here = head_width // HD
    hidden = up_weight.shape[1]
    hidden_piece = hidden // units
    slot_count = rows * parts
    qkv_width = 3 * head_width

    spans = jnp.stack([(ring.own - k) % parts for k in range(parts)])
    slots = (spans[:, None] * rows + jnp.arange(rows)[None, :]).reshape(slot_count)
    slots = slots.astype(jnp.int32)
    sequence_ids = ids_at(lengths, seq_owner, lax.axis_index("dp"), slots)
    positions = slots.astype(f32)
    live_rows = (sequence_ids[:rows] > 0).astype(f32)[:, None]
    qkv_flat = qkv_weight.reshape(width, qkv_width)
    qkv_shift = jnp.concatenate([qkv_bias[0], jnp.zeros((head_width,), f32), qkv_bias[1]])
    head_numbers = ring.own * heads_here + jnp.arange(heads_here) + 1
    slopes = jnp.exp2(-8.0 * head_numbers.astype(f32) / HEADS)

    input_float = block_input.astype(f32)
    normed1, inv_std1 = normalize(input_float)
    normed1_all = jnp.concatenate(ring.gather(normed1.astype(bf16)), axis=0)

    grad_out = live_rows * cotangent.astype(f32)
    grad_out_all = jnp.concatenate(plane.gather(grad_out.astype(bf16)), axis=0)

    out_rows = head_width // group
    out_piece = lax.dynamic_slice_in_dim(out_weight, plane.member * out_rows, out_rows)
    out_pieces = jnp.stack(ring.gather(out_piece), axis=0)
    out_pieces = [p.reshape(parts * out_rows, width) for p in plane.gather_pieces(out_pieces)]
    out_whole = jnp.zeros((parts, group, out_rows, width), bf16)
    for k, piece in enumerate(out_pieces):
        out_whole = lax.dynamic_update_slice(
            out_whole,
            piece.reshape(parts, 1, out_rows, width),
            (0, plane.member ^ k, 0, 0),
        )
    out_whole = out_whole.reshape(parts * head_width, width)

    norm1_all = (normed1_all.astype(f32) * norm1_gain + norm1_bias).astype(bf16)
    projected = (dot_plain(norm1_all, qkv_flat) + qkv_shift).astype(bf16)
    projected = projected.reshape(slot_count, 3, heads_here, HD)
    query, keys, values = (projected[:, 0], projected[:, 1], projected[:, 2])
    context, log_total = attend(query, keys, values, slopes, positions, sequence_ids)
    context = context.reshape(slot_count, head_width)
    context_rows = jnp.concatenate(
        ring.scatter([context[k * rows : (k + 1) * rows] for k in range(parts)]), axis=1
    )

    up_piece = lax.dynamic_slice_in_dim(up_weight, plane.unit * hidden_piece, hidden_piece, 1).T
    down_piece = lax.dynamic_slice_in_dim(down_weight, plane.unit * hidden_piece, hidden_piece)
    bias_piece = lax.dynamic_slice_in_dim(up_bias, plane.unit * hidden_piece, hidden_piece)
    bias_high = lax.reduce_precision(bias_piece, 8, 7)
    bias_rows = jnp.pad(
        jnp.stack([bias_high, bias_piece - bias_high]).astype(bf16),
        ((0, 14), (0, width - hidden_piece)),
    )
    own_piece, other_piece = plane.core_parts((up_piece, down_piece))
    own_piece = after(own_piece, normed1_all)
    if plane.cores == 2:
        mine = ring.gather(jnp.concatenate([own_piece, bias_rows], axis=0))
        bias_got = [m[hidden_piece : hidden_piece + 2] for m in mine]
        mine = [m[:hidden_piece] for m in mine]
        theirs = [other_piece] + [plane.swap(m) for m in mine[1:]]
    else:
        both = ring.gather(jnp.concatenate([own_piece, other_piece, bias_rows], axis=0))
        bias_got = [b[2 * hidden_piece : 2 * hidden_piece + 2] for b in both]
        mine = [b[:hidden_piece] for b in both]
        theirs = [b[hidden_piece : 2 * hidden_piece] for b in both]
    mine, theirs = jnp.concatenate(mine, axis=0), jnp.concatenate(theirs, axis=0)
    up_whole, down_whole = plane.core_parts((mine, theirs))
    bias_whole = jnp.concatenate(
        [jnp.sum(b[:, :hidden_piece].astype(f32), axis=0) for b in bias_got]
    )

    residual = input_float + (dot_plain(context_rows, out_whole) + out_bias)
    normed2, inv_std2 = normalize(residual)
    norm2_out = (normed2 * norm2_gain + norm2_bias).astype(bf16)
    norm2_all = jnp.concatenate(plane.gather(norm2_out), axis=0)

    value, slope = gelu_both(dot_last(norm2_all, up_whole) + bias_whole)
    activated = value.astype(bf16)
    pre_grad = (dot_last(grad_out_all, down_whole) * slope).astype(bf16)

    def unit_rows(array, k):
        return array[k * rows : (k + 1) * rows]

    norm2_grad = plane.sum_blocks(
        [dot_plain(unit_rows(pre_grad, k), up_whole) for k in range(units)]
    )

    grad_up = dot_first(pre_grad, norm2_all)
    grad_down = dot_first(activated, grad_out_all)
    grad_up_bias = jnp.sum(pre_grad.astype(f32), axis=0)
    keep, give = plane.core_parts((grad_up, grad_down))
    if plane.cores == 2:
        keep = keep + plane.swap(give.astype(bf16)).astype(f32)
    else:
        keep = jnp.concatenate(
            [
                keep.reshape(parts, hidden_piece, width),
                give.reshape(parts, hidden_piece, width),
            ],
            axis=1,
        ).reshape(parts * 2 * hidden_piece, width)
    block = keep.shape[0] // parts
    ffn_piece = sum_ring(ring, [keep[k * block : (k + 1) * block] for k in range(parts)])
    ffn_pieces = plane.gather(plane.outer_sum(ffn_piece).astype(bf16))
    if plane.cores == 2:
        far = [plane.swap(piece) for piece in ffn_pieces]
        ups, downs = zip(*[plane.core_parts(pair) for pair in zip(ffn_pieces, far)])
    else:
        ups = [piece[:hidden_piece] for piece in ffn_pieces]
        downs = [piece[hidden_piece:] for piece in ffn_pieces]
    grad_down_weight = plane.in_order(downs, plane.unit, lambda p: p.astype(f32))
    grad_up_weight = plane.in_order(ups, plane.unit, lambda p: p).T.astype(f32)

    resid_grad = grad_out + norm_back(norm2_grad, normed2, inv_std2, norm2_gain)
    resid_grad_bf = resid_grad.astype(bf16)

    context_grad = dot_last(resid_grad_bf, out_whole).astype(bf16)
    context_grad = jnp.concatenate(
        ring.scatter(
            [context_grad[:, k * head_width : (k + 1) * head_width] for k in range(parts)]
        ),
        axis=0,
    ).reshape(slot_count, heads_here, HD)
    query_grad, key_grad, value_grad = attend_back(
        query, keys, values, slopes, positions, sequence_ids, log_total, context_grad
    )
    qkv_grad = jnp.concatenate(
        [g.reshape(slot_count, head_width) for g in (query_grad, key_grad, value_grad)], axis=1
    )
    norm1_grad = sum_ring(
        ring, [dot_last(unit_rows(qkv_grad, k), qkv_flat) for k in range(parts)]
    )
    input_grad = (resid_grad + norm_back(norm1_grad, normed1, inv_std1, norm1_gain)).astype(bf16)

    ffn_blocks = [dot_plain(unit_rows(activated, k), down_whole) for k in range(units)]
    ffn_out = plane.sum_blocks(ffn_blocks)
    block_output = (live_rows * (residual + (ffn_out + down_bias))).astype(bf16)

    width_piece = width // group
    grad_out_weight = dot_first(resid_grad_bf, context_rows)
    out_grad = plane.reduce_pieces(
        grad_out_weight.reshape(group, width_piece, parts * head_width)
    )
    out_grad = sum_ring(
        ring, [out_grad[:, k * head_width : (k + 1) * head_width] for k in range(parts)]
    )

    qkv_sums = jnp.sum(qkv_grad.astype(f32), axis=0)
    correlation = dot_first(normed1_all, qkv_grad)
    grad_qkv = norm1_gain[:, None] * correlation + norm1_bias[:, None] * qkv_sums[None, :]
    qkv_float = qkv_flat.astype(f32)
    grad_norm1_gain = jnp.sum(qkv_float * correlation, axis=1)
    grad_norm1_bias = jnp.sum(qkv_float * qkv_sums[None, :], axis=1)
    qkv_piece = plane.reduce_pieces(grad_qkv.reshape(group, width_piece, qkv_width))

    shared = jnp.stack(
        [
            grad_norm1_gain,
            grad_norm1_bias,
            jnp.sum(resid_grad, axis=0),
            jnp.sum(norm2_grad * normed2, axis=0),
            jnp.sum(norm2_grad, axis=0),
            jnp.sum(grad_out, axis=0),
        ]
    )
    small_rows = 8
    up_rows = jnp.pad(
        grad_up_bias.reshape(parts, 1, hidden_piece), ((0, 0), (0, 1), (0, width - hidden_piece))
    )
    small = sum(
        ring.scatter([jnp.concatenate([shared, up_rows[k]], axis=0) for k in range(parts)])
    )
    bias_sums = jnp.concatenate([qkv_sums[:head_width], qkv_sums[2 * head_width :]])
    small = small.at[small_rows - 1, : 2 * head_width].set(bias_sums)

    tail = jnp.concatenate(
        [
            plane.outer_sum(qkv_piece).astype(bf16),
            plane.outer_sum(out_grad).astype(bf16),
            plane.outer_sum(small).astype(bf16).reshape(width_piece, small_rows * group),
        ],
        axis=1,
    )
    tails = plane.gather_pieces(tail)
    merged = plane.in_order(tails, plane.member, lambda p: p)
    grad_qkv_weight = merged[:, :qkv_width].astype(f32).reshape(width, 3, head_width)
    grad_out_weight = merged[:, qkv_width : qkv_width + head_width].T.astype(f32)
    smalls = merged[:, qkv_width + head_width :].astype(f32).reshape(group, small_rows, width)
    totals = jnp.sum(smalls, axis=0)
    up_sums = smalls[:, small_rows - 2, :hidden_piece].reshape(units, plane.cores, hidden_piece)
    grad_up_bias = jnp.sum(up_sums, axis=1).reshape(hidden)
    grad_qkv_bias = totals[small_rows - 1, : 2 * head_width].reshape(2, head_width)
    return (
        block_output,
        input_grad,
        totals[0],
        totals[1],
        grad_qkv_weight,
        grad_qkv_bias,
        grad_out_weight,
        totals[2],
        totals[3],
        totals[4],
        grad_up_weight,
        grad_up_bias,
        grad_down_weight,
        totals[5],
    )


def solution(mesh):
    return jax.shard_map(
        shards,
        mesh=mesh,
        in_specs=(
            P(("dp", "tensor"), None),
            P(),
            P(),
            P(None, None, "tensor"),
            P(None, "tensor"),
            P("tensor", None),
            P(),
            P(),
            P(),
            P(None, "tensor"),
            P("tensor"),
            P("tensor", None),
            P(),
            P(),
            P(),
            P(("dp", "tensor"), None),
        ),
        out_specs=(
            P(("dp", "tensor"), None),
            P(("dp", "tensor"), None),
            P(),
            P(),
            P(None, None, "tensor"),
            P(None, "tensor"),
            P("tensor", None),
            P(),
            P(),
            P(),
            P(None, "tensor"),
            P("tensor"),
            P("tensor", None),
            P(),
        ),
        check_vma=False,
    )
```
